32 devices in a mesh: slide: 4 (over y, x), seq: 8 (over z, core).
Axes of the slice: x: 2, y: 2, z: 4, core: 2. Of those that a mesh axis runs over, the one named last changes fastest.
Arguments:
- embeds: bfloat16 [12288, 1536], P(('slide', 'seq'))
- destination: int32 [12288, 1], P(('slide', 'seq')), may hold values from 0 to 31; in each aligned block of 384 rows (0 to 383, 384 to 767, ...) at most 24 rows name the same one
- norm_gain: float32 [1536], replicated, may hold values from 0.1 to 1.9
- qkv_weight: bfloat16 [1536, 4608], replicated
- out_weight: bfloat16 [1536, 1536], replicated, may hold values from -0.15625 to 0.15625
- finding_queries: bfloat16 [256, 1536], replicated
Outputs:
- layer_out: bfloat16 [24576, 1536], P(('slide', 'seq'))
- heatmap: float32 [24576, 256], P(('slide', 'seq'))
The draws below stay inside these ranges and needn't reach their ends.
Inputs may be any that keep to these rules, and one draw needn't show every extreme that they name: `destination`: each block of 384 rows (one encoder device) names any one device at most 24 times, and some block names some device exactly 24 times; every device is named by some row.
All inputs are finite; a program needn't handle non-finite values.
Results may differ from the reference program's by a relative error of at most 0.01225.
The reference program's roundings to bfloat16 on the way (of `tiles`, `normed`, `projected`, `weights`, `mixed` and `keys_find`) count: a program that leaves them out, or rounds other values in their place, can miss the bound.
Values may be sent and summed in bfloat16 or wider, within the bound.
A program may use at most 192 MiB of HBM per device.

```python
import math
import jax
import jax.numpy as jnp
import numpy as np
from jax import lax

D = 1536
HEADS = 12
HEAD_DIM = 128
FIND = 256
TOK_DEV = 768
PAIR_CAP = 24
ENC_DEV = 384
ENC_ROWS = 12288
SLOTS = 24576
SLIDE_LEN = 6144
SLIDES = 4
DEVICES = 32


def draw_embeds(key, part):
    value_key = jax.random.fold_in(key, 11)
    blank_key = jax.random.fold_in(key, 12)
    values_drawn = jnp.clip(jax.random.normal(value_key, (ENC_ROWS, D), jnp.float32), -6.0, 6.0)
    present_row = jax.random.randint(blank_key, (ENC_ROWS, 1), 0, 16) != 0
    return jnp.where(present_row, values_drawn, 0.0).astype(jnp.bfloat16)


def draw_qkv_weight(key, part):
    return (jax.random.normal(key, (D, 3 * D), jnp.float32) * D ** (-0.5)).astype(jnp.bfloat16)


def draw_finding_queries(key, part):
    return jax.random.normal(key, (FIND, D), jnp.float32).astype(jnp.bfloat16)


def routed_block(stream_key, own, number, rows, amount, top, limit, lean):
    order = jax.random.permutation(stream_key, amount)
    crowded, usual = load_shares(amount, rows * top, limit, lean, True), load_shares(amount, rows * top, limit, lean, False)
    places = jnp.arange(amount)

    def named(tallies, turn):
        used = int((tallies > 0).sum())
        fixed = max(1, used // 4)
        shifted = fixed + (places - fixed + turn * (used - fixed)) % max(1, amount - fixed)
        return jnp.zeros((amount,), jnp.int32).at[order[jnp.where(places < fixed, places, shifted)]].set(jnp.asarray(tallies, jnp.int32))

    tallies = jnp.where(number % 4 == 0, named(crowded, number // 4), named(usual, number - number // 4 - 1))
    mixed = jax.random.permutation(jax.random.fold_in(own, 3), amount)
    donor, taker = mixed[0:amount // 2 * 2:2], mixed[1:amount // 2 * 2:2]
    margin = jnp.minimum(tallies[donor] - 1, limit - tallies[taker]) // 2
    margin = jnp.where((donor == order[0]) | (taker == order[0]) | (tallies[taker] == 0), 0, jnp.maximum(margin, 0))
    shifted = jax.random.randint(jax.random.fold_in(own, 4), (amount // 2,), 0, 1 << 20) % (margin + 1)
    tallies = tallies.at[donor].add(-shifted).at[taker].add(shifted)
    members = jnp.searchsorted(jnp.cumsum(tallies), jnp.arange(rows * top), side="right").astype(jnp.int32)
    grid = members.reshape(top, rows).T
    grid = grid[jax.random.permutation(jax.random.fold_in(own, 1), rows)]
    turn = jax.random.randint(jax.random.fold_in(own, 2), (rows, 1), 0, top)
    return jnp.take_along_axis(grid, (jnp.arange(top)[None, :] + turn) % top, axis=1)


def load_shares(amount, total, reach, slope, full):
    loads = [(1 << 20) // math.isqrt(rank ** slope) + 1 for rank in range(1, amount + 1)]
    largest = reach if full else min(reach, max(-(-total // amount), total * loads[0] // sum(loads)))
    least = 1 if total - largest >= amount - 1 else 0
    given, rest = [largest] + [least] * (amount - 1), total - largest - least * (amount - 1)
    while rest > 0:
        free = [i for i in range(1, amount) if given[i] < largest] or [i for i in range(1, amount) if given[i] < reach]
        whole, budget = sum([loads[i] for i in free]), rest
        for i in free:
            more = min(reach - given[i], max(1, budget * loads[i] // whole), rest)
            given[i] = given[i] + more
            rest = rest - more
    return np.array(given)


def scatter_about(own_key, shape, width, most, kind=jnp.bfloat16):
    return jnp.clip(width * jax.random.normal(own_key, shape, jnp.float32), -most, most).astype(kind)


def setup_inputs(seed: int = 0) -> dict:
    key_of = jax.random.split(jax.random.key(seed), 7)
    embeds = draw_embeds(jax.random.fold_in(key_of[6], 71), 0)
    destination_keys = jax.random.split(jax.random.fold_in(key_of[1], 1), ENC_ROWS // ENC_DEV)
    destination_turns = jax.random.permutation(jax.random.fold_in(key_of[1], 3), ENC_ROWS // ENC_DEV)
    destination = jax.vmap(lambda own, number: routed_block(jax.random.fold_in(key_of[1], 2), own, number, ENC_DEV, DEVICES, 1, PAIR_CAP, 2))(destination_keys, destination_turns).reshape((ENC_ROWS, 1))
    norm_gain = jnp.clip(1.0 + 0.18 * jax.random.normal(key_of[2], (D,), jnp.float32), 0.1, 1.9)
    qkv_weight = draw_qkv_weight(jax.random.fold_in(key_of[6], 71), 0)
    out_weight = scatter_about(key_of[4], (D, D), D ** -0.5, 0.15625)
    finding_queries = draw_finding_queries(jax.random.fold_in(key_of[6], 71), 0)
    return dict(embeds=embeds, destination=destination, norm_gain=norm_gain, qkv_weight=qkv_weight, out_weight=out_weight, finding_queries=finding_queries)


MASKED = -1e+30
EPSILON = 1e-06

def choose_heads(rate, spread):
    return jnp.arange(rate)[:, None] == jnp.arange(HEADS)[None, :] // spread % rate

def select(rows, rate, spread):
    count = rows.shape[0]
    grouped = rows.reshape(count // rate, rate, rows.shape[1], rows.shape[2])
    chosen = choose_heads(rate, spread)
    return lax.optimization_barrier(jnp.sum(jnp.where(chosen[None, :, :, None], grouped, jnp.zeros((), rows.dtype)), axis=1))

def spread_back(rows, rate, fill):
    count = rows.shape[0]
    chosen = choose_heads(rate, 1)
    widened = jnp.where(chosen[None, :, :, None], rows[:, None], jnp.asarray(fill, rows.dtype))
    return widened.reshape(count * rate, rows.shape[1], rows.shape[2])

def attend_exact(query, key_rows, value, keep):
    scale = query.shape[-1] ** (-0.5)
    scores = jnp.einsum('qhe,khe->hqk', query.astype(jnp.float32), key_rows.astype(jnp.float32)) * scale
    allowed = (keep[:, :, 0] > 0.5).T[:, None, :]
    scores = jnp.where(allowed, scores, MASKED)
    peak = lax.optimization_barrier(jnp.max(scores, axis=2, keepdims=True))
    exp_scores = jnp.where(allowed, jnp.exp(scores - peak), 0.0)
    total = lax.optimization_barrier(jnp.sum(exp_scores, axis=2))
    rounded = exp_scores.astype(jnp.bfloat16)
    weights = lax.optimization_barrier(rounded).astype(jnp.float32)
    weighted = jnp.einsum('hqk,khe->qhe', weights, value.astype(jnp.float32))
    bounded = jnp.maximum(total, 1.0)
    result = weighted / bounded.T[:, :, None]
    log_total = jnp.where(total > 0.0, peak[:, :, 0] + jnp.log(bounded), MASKED).T[:, :, None]
    return (result, log_total)

def arrange(embeds, destination):
    target = destination[:, 0].reshape(DEVICES, ENC_DEV)
    one_hot = (target[:, :, None] == jnp.arange(DEVICES, dtype=jnp.int32)[None, None, :]).astype(jnp.int32)
    rank = lax.optimization_barrier(jnp.sum(jnp.cumsum(one_hot, axis=1) * one_hot, axis=2)) - 1
    source = jnp.arange(DEVICES, dtype=jnp.int32)[:, None]
    place = (target * TOK_DEV + source * PAIR_CAP + rank).reshape(-1).astype(jnp.int32)
    tiles = jnp.zeros((SLOTS, D), jnp.bfloat16).at[place].set(embeds)
    valid = jnp.zeros((SLOTS,), jnp.int32).at[place].set(1)
    return (tiles, valid)

def one_slide(tiles, valid, norm_gain, qkv_weight, out_weight, finding_queries):
    tile_f32 = tiles.astype(jnp.float32)
    normed = (tile_f32 * lax.rsqrt(lax.optimization_barrier(jnp.mean(tile_f32 * tile_f32, axis=1, keepdims=True)) + EPSILON) * norm_gain).astype(jnp.bfloat16)
    projected = jnp.dot(normed, qkv_weight, preferred_element_type=jnp.float32).astype(jnp.bfloat16)
    projected = projected.reshape(SLIDE_LEN, 3, HEADS, HEAD_DIM)
    query, key_rows, value = (projected[:, 0], projected[:, 1], projected[:, 2])
    keep = jnp.broadcast_to(valid.astype(jnp.float32)[:, None, None], (SLIDE_LEN, HEADS, 1))
    results = []
    logs = []
    for rate in (1, 2, 4):
        picked = [select(member, rate, 1) for member in (query, key_rows, value, keep)]
        segments = picked[0].shape[0] // TOK_DEV
        shaped = tuple((member.reshape(segments, TOK_DEV, HEADS, member.shape[-1]) for member in picked))
        branch, log_total = lax.map(lambda pack: attend_exact(pack[0], pack[1], pack[2], pack[3]), shaped)
        results.append(spread_back(branch.reshape(-1, HEADS, HEAD_DIM), rate, 0.0))
        logs.append(spread_back(log_total.reshape(-1, HEADS, 1), rate, MASKED))
    stacked = jnp.stack(logs)
    top = lax.optimization_barrier(jnp.max(stacked, axis=0))
    factors = jnp.exp(stacked - top)
    mixed = (factors[0] * results[0] + factors[1] * results[1] + factors[2] * results[2]) / lax.optimization_barrier(jnp.sum(factors, axis=0))
    mixed = mixed.astype(jnp.bfloat16).reshape(SLIDE_LEN, D)
    layer_out = (tile_f32 + jnp.dot(mixed, out_weight, preferred_element_type=jnp.float32)).astype(jnp.bfloat16)
    out_f32 = layer_out.astype(jnp.float32)
    keys_find = (out_f32 * lax.rsqrt(lax.optimization_barrier(jnp.mean(out_f32 * out_f32, axis=1, keepdims=True)) + EPSILON)).astype(jnp.bfloat16)
    keys_find = keys_find.reshape(SLIDE_LEN, HEADS, HEAD_DIM).astype(jnp.float32)
    queries_find = finding_queries.reshape(FIND, HEADS, HEAD_DIM).astype(jnp.float32)
    scores = jnp.einsum('fhe,the->hft', queries_find, keys_find) * HEAD_DIM ** (-0.5)
    allowed = (valid > 0)[None, None, :]
    scores = jnp.where(allowed, scores, MASKED)
    peak = lax.optimization_barrier(jnp.max(scores, axis=2, keepdims=True))
    exp_scores = jnp.where(allowed, jnp.exp(scores - peak), 0.0)
    probs = exp_scores / lax.optimization_barrier(jnp.sum(exp_scores, axis=2, keepdims=True))
    heat = lax.optimization_barrier(jnp.sum(probs, axis=0)).T * (SLIDE_LEN / HEADS)
    return (layer_out, heat)

def reference(embeds, destination, norm_gain, qkv_weight, out_weight, finding_queries):
    tiles, valid = arrange(embeds, destination)
    tiles_slides = tiles.reshape(SLIDES, SLIDE_LEN, D)
    valid_slides = valid.reshape(SLIDES, SLIDE_LEN)
    layer_out, heat = lax.map(lambda pack: one_slide(pack[0], pack[1], norm_gain, qkv_weight, out_weight, finding_queries), (tiles_slides, valid_slides))
    return (layer_out.reshape(SLOTS, D), heat.reshape(SLOTS, FIND))
```

```python
import functools
import math

import jax
import jax.numpy as jnp
from jax import lax
from jax.experimental import pallas as pl
from jax.experimental.pallas import tpu as pltpu
from jax.sharding import PartitionSpec as P

HEADS = 12
HEAD = 128
GROUP = 4
WIDE = GROUP * HEAD
MASKED = -1e30
EPSILON = 1e-06
FACTOR = math.log2(math.e) / math.sqrt(HEAD)
F32 = jnp.float32
BF16 = jnp.bfloat16
QUARTER_OF = (0, 2, 1, 3)
VMEM_LIMIT = 56 * 1024 * 1024


def params(**more):
    return pltpu.CompilerParams(vmem_limit_bytes=VMEM_LIMIT, **more)


def dispatch_kernel(capacity, col_ref, row_ref, embeds_ref, buffer_ref, counts_ref):
    rows = embeds_ref.shape[0]
    slots = buffer_ref.shape[0]
    col = col_ref[...]
    row = row_ref[...]
    first = lax.broadcasted_iota(jnp.int32, (rows, rows), 0)
    second = lax.broadcasted_iota(jnp.int32, (rows, rows), 1)
    same = jnp.logical_and(col == row, first < second)
    rank = jnp.sum(same.astype(F32), axis=0, keepdims=True).astype(jnp.int32)
    place = row * capacity + rank
    lanes = lax.broadcasted_iota(jnp.int32, (rows, counts_ref.shape[1]), 1)
    counts_ref[...] = jnp.sum((col == lanes).astype(F32), axis=0, keepdims=True).astype(jnp.int32)
    chosen = (lax.broadcasted_iota(jnp.int32, (slots, rows), 0) == place).astype(F32).astype(BF16)
    for start in range(0, embeds_ref.shape[1], WIDE):
        part = embeds_ref[:, start : start + WIDE]
        buffer_ref[:, start : start + WIDE] = jnp.dot(
            chosen, part, preferred_element_type=F32
        ).astype(BF16)


def dispatch(destination, embeds, devices, capacity):
    rows, width = embeds.shape
    slots = devices * capacity
    return pl.pallas_call(
        functools.partial(dispatch_kernel, capacity),
        out_shape=(
            jax.ShapeDtypeStruct((slots, width), BF16),
            jax.ShapeDtypeStruct((1, max(128, devices)), jnp.int32),
        ),
        compiler_params=params(),
        name="dispatch",
    )(destination, destination.reshape(1, rows), embeds)


def original_of(index, quarter):
    block = (
        (index >= quarter).astype(jnp.int32)
        + (index >= 2 * quarter).astype(jnp.int32)
        + (index >= 3 * quarter).astype(jnp.int32)
    )
    phase = 2 * jnp.where((block == 1) | (block == 3), 1, 0) + (block >= 2).astype(jnp.int32)
    return 4 * (index - quarter * block) + phase


def project_kernel(tiles_ref, gain_ref, weight_ref, out_ref, near_ref, far_ref, normed_ref):
    step = pl.program_id(0)
    slots, width = tiles_ref.shape
    quarter = slots // 4
    half = slots // 2

    @pl.when(step == 0)
    def _():
        tile = tiles_ref[...].astype(F32)
        mean = jnp.mean(tile * tile, axis=1, keepdims=True)
        normed = (tile * lax.rsqrt(mean + EPSILON) * gain_ref[...]).astype(BF16)
        index = lax.broadcasted_iota(jnp.int32, (slots, slots), 0)
        position = lax.broadcasted_iota(jnp.int32, (slots, slots), 1)
        order = (original_of(index, quarter) == position).astype(F32).astype(BF16)
        for start in range(0, width, WIDE):
            normed_ref[:, start : start + WIDE] = jnp.dot(
                order, normed[:, start : start + WIDE], preferred_element_type=F32
            ).astype(BF16)

    value = jnp.dot(normed_ref[...], weight_ref[...], preferred_element_type=F32).astype(BF16)
    out_ref[...] = value

    @pl.when(step >= 3)
    def _():
        for j in range(GROUP):
            cols = slice(j * HEAD, (j + 1) * HEAD)
            near_ref[:, cols] = value[(j % 2) * half : (j % 2 + 1) * half, cols]
            begin = QUARTER_OF[j] * quarter
            far_ref[:, cols] = value[begin : begin + quarter, cols]


def project(tiles, gain, weight):
    slots, width = tiles.shape
    steps = weight.shape[1] // WIDE
    tail = lambda i: (0, jnp.maximum(i - steps // 3, 0))
    return pl.pallas_call(
        project_kernel,
        grid=(steps,),
        in_specs=[
            pl.BlockSpec((slots, width), lambda i: (0, 0)),
            pl.BlockSpec((1, width), lambda i: (0, 0)),
            pl.BlockSpec((width, WIDE), lambda i: (0, i)),
        ],
        out_specs=[
            pl.BlockSpec((slots, WIDE), lambda i: (0, i)),
            pl.BlockSpec((slots // 2, WIDE), tail),
            pl.BlockSpec((slots // 4, WIDE), tail),
        ],
        out_shape=(
            jax.ShapeDtypeStruct((slots, 3 * width), BF16),
            jax.ShapeDtypeStruct((slots // 2, 2 * width), BF16),
            jax.ShapeDtypeStruct((slots // 4, 2 * width), BF16),
        ),
        scratch_shapes=[pltpu.VMEM((slots, width), BF16)],
        compiler_params=params(),
        cost_estimate=pl.CostEstimate(
            flops=2 * slots * width * 3 * width, bytes_accessed=30_000_000, transcendentals=0
        ),
        name="project",
    )(tiles, gain.reshape(1, width), weight)


def softmax_parts(query, keys, values, bias):
    scores = lax.dot_general(
        query, keys, (((1,), (1,)), ((), ())), preferred_element_type=F32
    )
    scores = scores * FACTOR + bias
    peak = jnp.max(scores, axis=1, keepdims=True)
    weights = jnp.exp2(scores - peak)
    total = jnp.sum(weights, axis=1, keepdims=True)
    summed = jnp.dot(weights.astype(BF16), values, preferred_element_type=F32)
    return summed, peak, total


def near_attention_kernel(q_ref, k_ref, v_ref, bias_ref, summed_ref, stats_ref):
    slots = q_ref.shape[0]
    half = slots // 2
    lanes = lax.broadcasted_iota(jnp.int32, (half, HEAD), 1)
    bias = bias_ref[0:1, :]
    for part in range(2):
        rows = slice(part * half, (part + 1) * half)
        stats = jnp.zeros((half, HEAD), F32)
        for j in range(GROUP):
            cols = slice(j * HEAD, (j + 1) * HEAD)
            summed, peak, total = softmax_parts(q_ref[rows, cols], k_ref[:, cols], v_ref[:, cols], bias)
            summed_ref[rows, cols] = summed
            stats = jnp.where(lanes == 2 * j, peak, jnp.where(lanes == 2 * j + 1, total, stats))
        stats_ref[rows, :] = stats


def near_attention(projected, bias):
    slots, triple = projected.shape
    width = triple // 3
    steps = width // WIDE
    return pl.pallas_call(
        near_attention_kernel,
        grid=(steps,),
        in_specs=[
            pl.BlockSpec((slots, WIDE), lambda i: (0, i)),
            pl.BlockSpec((slots, WIDE), lambda i: (0, i + steps)),
            pl.BlockSpec((slots, WIDE), lambda i: (0, i + 2 * steps)),
            pl.BlockSpec(bias.shape, lambda i: (0, 0)),
        ],
        out_specs=[
            pl.BlockSpec((slots, WIDE), lambda i: (0, i)),
            pl.BlockSpec((slots, HEAD), lambda i: (0, i)),
        ],
        out_shape=(
            jax.ShapeDtypeStruct((slots, width), F32),
            jax.ShapeDtypeStruct((slots, steps * HEAD), F32),
        ),
        compiler_params=params(),
        cost_estimate=pl.CostEstimate(
            flops=8 * slots * slots * width,
            bytes_accessed=14_000_000,
            transcendentals=4 * slots * slots * HEADS,
        ),
        name="near_attention",
    )(projected, projected, projected, bias)


def combine(parts):
    top = parts[0][1]
    for _, peak, _ in parts[1:]:
        top = jnp.maximum(top, peak)
    above, below = 0.0, 0.0
    for summed, peak, total in parts:
        factor = jnp.exp2(peak - top)
        above = above + factor * summed
        below = below + factor * total
    return (above * (1.0 / jnp.maximum(below, 1.0))).astype(BF16)


def far_attention_kernel(
    q_ref, k_ref, v_ref, bias_ref, pair_k, pair_v, one_k, one_v, two_k, two_v,
    summed_ref, stats_ref, mixed_ref,
):
    slots = q_ref.shape[0]
    half, quarter = slots // 2, slots // 4
    for j in range(GROUP):
        cols = slice(j * HEAD, (j + 1) * HEAD)
        start = (j % 2) * half
        begin = QUARTER_OF[j] * quarter
        inside = begin - start
        mine = slice(start, start + half)
        fourth = slice(begin, begin + quarter)
        within = slice(inside, inside + quarter)

        def local(rows):
            return (
                summed_ref[rows, cols],
                stats_ref[rows, 2 * j : 2 * j + 1],
                stats_ref[rows, 2 * j + 1 : 2 * j + 2],
            )

        keys = jnp.concatenate([k_ref[mine, cols], pair_k[:, cols]], axis=0)
        values = jnp.concatenate([v_ref[mine, cols], pair_v[:, cols]], axis=0)
        two = softmax_parts(q_ref[mine, cols], keys, values, bias_ref[1 + j % 2 : 2 + j % 2, :])
        keys = jnp.concatenate(
            [k_ref[fourth, cols], pair_k[within, cols], one_k[:, cols], two_k[:, cols]], axis=0
        )
        values = jnp.concatenate(
            [v_ref[fourth, cols], pair_v[within, cols], one_v[:, cols], two_v[:, cols]], axis=0
        )
        four = softmax_parts(q_ref[fourth, cols], keys, values, bias_ref[3 + j : 4 + j, :])
        other = slice(half - start, 2 * half - start)
        mixed_ref[other, cols] = combine([local(other)])
        for offset in (0, quarter):
            rows = slice(start + offset, start + offset + quarter)
            parts = [local(rows), tuple(x[offset : offset + quarter] for x in two)]
            if offset == inside:
                parts.append(four)
            mixed_ref[rows, cols] = combine(parts)


def far_attention(projected, bias, pair, one, two, summed, stats):
    slots, triple = projected.shape
    width = triple // 3
    steps = width // WIDE

    def twice(array):
        rows = array.shape[0]
        return [
            pl.BlockSpec((rows, WIDE), lambda i: (0, i)),
            pl.BlockSpec((rows, WIDE), lambda i: (0, i + steps)),
        ]

    return pl.pallas_call(
        far_attention_kernel,
        grid=(steps,),
        in_specs=[
            pl.BlockSpec((slots, WIDE), lambda i: (0, i)),
            pl.BlockSpec((slots, WIDE), lambda i: (0, i + steps)),
            pl.BlockSpec((slots, WIDE), lambda i: (0, i + 2 * steps)),
            pl.BlockSpec(bias.shape, lambda i: (0, 0)),
            *twice(pair),
            *twice(one),
            *twice(two),
            pl.BlockSpec((slots, WIDE), lambda i: (0, i)),
            pl.BlockSpec((slots, HEAD), lambda i: (0, i)),
        ],
        out_specs=pl.BlockSpec((slots, WIDE), lambda i: (0, i)),
        out_shape=jax.ShapeDtypeStruct((slots, width), BF16),
        compiler_params=params(),
        name="far_attention",
    )(projected, projected, projected, bias, pair, pair, one, one, two, two, summed, stats)


def finish_kernel(mixed_ref, tiles_ref, weight_ref, finding_ref, mask_ref, layer_ref, keys_ref, stats_ref, plain_ref):
    slots, width = tiles_ref.shape
    quarter = slots // 4
    position = lax.broadcasted_iota(jnp.int32, (slots, slots), 0)
    index = lax.broadcasted_iota(jnp.int32, (slots, slots), 1)
    order = (original_of(index, quarter) == position).astype(F32).astype(BF16)
    for start in range(0, width, WIDE):
        plain_ref[:, start : start + WIDE] = jnp.dot(
            order, mixed_ref[:, start : start + WIDE], preferred_element_type=F32
        ).astype(BF16)
    square = jnp.zeros((slots, 1), F32)
    for start in range(0, width, WIDE):
        cols = slice(start, start + WIDE)
        added = jnp.dot(plain_ref[...], weight_ref[:, cols], preferred_element_type=F32)
        out = (tiles_ref[:, cols].astype(F32) + added).astype(BF16)
        layer_ref[:, cols] = out
        wide = out.astype(F32)
        square = square + jnp.sum(wide * wide, axis=1, keepdims=True)
    inverse = lax.rsqrt(square * (1.0 / width) + EPSILON)
    mask = mask_ref[...]
    for h in range(HEADS):
        cols = slice(h * HEAD, (h + 1) * HEAD)
        keys = (layer_ref[:, cols].astype(F32) * inverse).astype(BF16)
        keys_ref[:, cols] = keys
        scores = lax.dot_general(
            keys, finding_ref[:, cols], (((1,), (1,)), ((), ())), preferred_element_type=F32
        )
        scores = scores * FACTOR + mask
        peak = jnp.max(scores, axis=0, keepdims=True)
        stats_ref[h : h + 1, :] = peak
        stats_ref[HEADS + h : HEADS + h + 1, :] = jnp.sum(
            jnp.exp2(scores - peak), axis=0, keepdims=True
        )


def finish(mixed, tiles, weight, finding, mask):
    slots, width = tiles.shape
    return pl.pallas_call(
        finish_kernel,
        out_shape=(
            jax.ShapeDtypeStruct((slots, width), BF16),
            jax.ShapeDtypeStruct((slots, width), BF16),
            jax.ShapeDtypeStruct((2 * HEADS, finding.shape[0]), F32),
        ),
        scratch_shapes=[pltpu.VMEM((slots, width), BF16)],
        compiler_params=params(),
        name="finish",
    )(mixed, tiles, weight, finding, mask)


def heat_kernel(count, scale, stats_ref, keys_ref, finding_ref, mask_ref, heat_ref, held, send_sem, recv_sem):
    slide = lax.axis_index("slide")
    me = lax.axis_index("seq")
    barrier = pltpu.get_barrier_semaphore()
    for hop in range(1, count):
        peer = lax.rem(me + hop, count)
        pl.semaphore_signal(
            barrier, inc=1, device_id=(slide, peer), device_id_type=pl.DeviceIdType.MESH
        )
    pl.semaphore_wait(barrier, count - 1)
    copies = []
    for hop in range(1, count):
        peer = lax.rem(me + hop, count)
        copy = pltpu.make_async_remote_copy(
            src_ref=stats_ref,
            dst_ref=held.at[hop],
            send_sem=send_sem.at[hop],
            recv_sem=recv_sem.at[hop],
            device_id=(slide, peer),
            device_id_type=pl.DeviceIdType.MESH,
        )
        copy.start()
        copies.append(copy)
    for copy in copies:
        copy.wait()
    everything = [stats_ref[...]] + [held[hop] for hop in range(1, count)]
    peaks = everything[0][:HEADS]
    for part in everything[1:]:
        peaks = jnp.maximum(peaks, part[:HEADS])
    totals = jnp.zeros_like(peaks)
    for part in everything:
        totals = totals + part[HEADS:] * jnp.exp2(part[:HEADS] - peaks)
    factors = scale / totals
    slots = keys_ref.shape[0]
    chunk = slots // 2
    for start in range(0, slots, chunk):
        rows = slice(start, start + chunk)
        mask = mask_ref[rows, :]
        total = jnp.zeros((chunk, finding_ref.shape[0]), F32)
        for h in range(HEADS):
            cols = slice(h * HEAD, (h + 1) * HEAD)
            scores = lax.dot_general(
                keys_ref[rows, cols], finding_ref[:, cols], (((1,), (1,)), ((), ())),
                preferred_element_type=F32,
            )
            scores = scores * FACTOR + mask
            total = total + jnp.exp2(scores - peaks[h : h + 1]) * factors[h : h + 1]
        heat_ref[rows, :] = total


def heat_map(count, stats, keys, finding, mask):
    slots = keys.shape[0]
    finds = finding.shape[0]
    return pl.pallas_call(
        functools.partial(heat_kernel, count, count * slots / HEADS),
        in_specs=[pl.BlockSpec(memory_space=pltpu.VMEM)] * 4,
        out_specs=pl.BlockSpec(memory_space=pltpu.VMEM),
        out_shape=jax.ShapeDtypeStruct((slots, finds), F32),
        scratch_shapes=[
            pltpu.VMEM((count, 2 * HEADS, finds), F32),
            pltpu.SemaphoreType.DMA((count,)),
            pltpu.SemaphoreType.DMA((count,)),
        ],
        compiler_params=params(collective_id=0, has_side_effects=True),
        name="heat_map",
    )(stats, keys, finding, mask)


def exchange(value, mask):
    pairs = [(source, source ^ mask) for source in range(lax.axis_size("seq"))]
    return lax.ppermute(value, "seq", pairs)


def shards(embeds, destination, norm_gain, qkv_weight, out_weight, finding_queries):
    devices = lax.axis_size(("slide", "seq"))
    seq_count = lax.axis_size("seq")
    slots = embeds.shape[0] * 2
    capacity = slots // devices
    half, quarter = slots // 2, slots // 4
    buffer, counts = dispatch(destination, embeds, devices, capacity)
    counts = lax.all_gather(counts[0], ("slide", "seq"))[:, :devices]
    tiles = lax.all_to_all(buffer, ("slide", "seq"), split_axis=0, concat_axis=0, tiled=True)

    me = lax.axis_index(("slide", "seq"))
    wanted = (me ^ jnp.arange(4, dtype=jnp.int32))[:, None] == jnp.arange(devices, dtype=jnp.int32)
    reached = jnp.sum(jnp.where(wanted[:, None, :], counts[None], 0), axis=2)
    open_slots = jnp.arange(capacity, dtype=jnp.int32)[None, None, :] < reached[:, :, None]
    bias = jnp.where(open_slots, 0.0, MASKED).astype(F32).reshape(4, slots)
    mask = bias[0].reshape(slots, 1)
    phased = bias.reshape(4, quarter, 4).transpose(0, 2, 1)
    phased = jnp.stack([phased[:, 0], phased[:, 2], phased[:, 1], phased[:, 3]], axis=1)
    rows = [phased[0].reshape(slots)]
    for parity in range(2):
        rows.append(phased[:2, 2 * parity : 2 * parity + 2].reshape(slots))
    for phase in range(4):
        rows.append(phased[:, QUARTER_OF[phase]].reshape(slots))
    rows.append(rows[0])
    bias = jnp.stack(rows)

    projected, near, far = project(tiles, norm_gain, qkv_weight)
    one = exchange(far, 2)
    pair = exchange(near, 1)
    summed, stats = near_attention(projected, bias)
    two = exchange(one, 1)
    mixed = far_attention(projected, bias, pair, one, two, summed, stats)
    layer_out, keys, stats = finish(mixed, tiles, out_weight, finding_queries, mask)
    heat = heat_map(seq_count, stats, keys, finding_queries, mask)
    return (layer_out, heat)


def solution(mesh):
    in_specs = (P(("slide", "seq"), None), P(("slide", "seq"), None), P(), P(), P(), P())
    out_specs = (P(("slide", "seq"), None), P(("slide", "seq"), None))
    return jax.shard_map(shards, mesh=mesh, in_specs=in_specs, out_specs=out_specs, check_vma=False)
```

```python
import functools
import math

import jax
import jax.numpy as jnp
from jax import lax
from jax.experimental import pallas as pl
from jax.experimental.pallas import tpu as pltpu
from jax.sharding import PartitionSpec as P

HEADS = 12
HEAD = 128
GROUP = 4
WIDE = GROUP * HEAD
MASKED = -1e30
EPSILON = 1e-06
FACTOR = math.log2(math.e) / math.sqrt(HEAD)
F32 = jnp.float32
BF16 = jnp.bfloat16
QUARTER_OF = (0, 2, 1, 3)
VMEM_LIMIT = 56 * 1024 * 1024


def params(**more):
    return pltpu.CompilerParams(vmem_limit_bytes=VMEM_LIMIT, **more)


def dispatch_kernel(capacity, col_ref, row_ref, embeds_ref, buffer_ref, counts_ref):
    rows = embeds_ref.shape[0]
    slots = buffer_ref.shape[0]
    col = col_ref[...]
    row = row_ref[...]
    first = lax.broadcasted_iota(jnp.int32, (rows, rows), 0)
    second = lax.broadcasted_iota(jnp.int32, (rows, rows), 1)
    same = jnp.logical_and(col == row, first < second)
    rank = jnp.sum(same.astype(F32), axis=0, keepdims=True).astype(jnp.int32)
    place = row * capacity + rank
    lanes = lax.broadcasted_iota(jnp.int32, (rows, counts_ref.shape[1]), 1)
    counts_ref[...] = jnp.sum((col == lanes).astype(F32), axis=0, keepdims=True).astype(jnp.int32)
    chosen = (lax.broadcasted_iota(jnp.int32, (slots, rows), 0) == place).astype(F32).astype(BF16)
    for start in range(0, embeds_ref.shape[1], WIDE):
        part = embeds_ref[:, start : start + WIDE]
        buffer_ref[:, start : start + WIDE] = jnp.dot(
            chosen, part, preferred_element_type=F32
        ).astype(BF16)


def dispatch(destination, embeds, devices, capacity):
    rows, width = embeds.shape
    slots = devices * capacity
    return pl.pallas_call(
        functools.partial(dispatch_kernel, capacity),
        out_shape=(
            jax.ShapeDtypeStruct((slots, width), BF16),
            jax.ShapeDtypeStruct((1, max(128, devices)), jnp.int32),
        ),
        compiler_params=params(),
        name="dispatch",
    )(destination, destination.reshape(1, rows), embeds)


def original_of(index, quarter):
    block = (
        (index >= quarter).astype(jnp.int32)
        + (index >= 2 * quarter).astype(jnp.int32)
        + (index >= 3 * quarter).astype(jnp.int32)
    )
    phase = 2 * jnp.where((block == 1) | (block == 3), 1, 0) + (block >= 2).astype(jnp.int32)
    return 4 * (index - quarter * block) + phase


def route_kernel(devices, seq_count, buffer_ref, counts_ref, tiles_ref, all_ref, send, recv, count_send, count_recv, own_sem):
    me = lax.axis_index("slide") * seq_count + lax.axis_index("seq")
    barrier = pltpu.get_barrier_semaphore()

    def place_of(hop):
        peer = lax.rem(me + hop, devices)
        return peer, (peer // seq_count, lax.rem(peer, seq_count))

    def greet(hop, carry):
        pl.semaphore_signal(
            barrier, inc=1, device_id=place_of(hop)[1], device_id_type=pl.DeviceIdType.MESH
        )
        return carry

    lax.fori_loop(1, devices, greet, 0)
    pl.semaphore_wait(barrier, devices - 1)

    def copies(hop):
        peer, where = place_of(hop)
        rows = pltpu.make_async_remote_copy(
            src_ref=buffer_ref.at[peer],
            dst_ref=tiles_ref.at[me],
            send_sem=send.at[hop],
            recv_sem=recv.at[hop],
            device_id=where,
            device_id_type=pl.DeviceIdType.MESH,
        )
        count = pltpu.make_async_remote_copy(
            src_ref=counts_ref.at[0],
            dst_ref=all_ref.at[me],
            send_sem=count_send.at[hop],
            recv_sem=count_recv.at[hop],
            device_id=where,
            device_id_type=pl.DeviceIdType.MESH,
        )
        return rows, count

    def begin(hop, carry):
        for copy in copies(hop):
            copy.start()
        return carry

    def end(hop, carry):
        for copy in copies(hop):
            copy.wait()
        return carry

    own_rows = pltpu.make_async_copy(buffer_ref.at[me], tiles_ref.at[me], own_sem.at[0])
    own_count = pltpu.make_async_copy(counts_ref.at[0], all_ref.at[me], own_sem.at[1])
    lax.fori_loop(1, devices, begin, 0)
    own_rows.start()
    own_count.start()
    own_rows.wait()
    own_count.wait()
    lax.fori_loop(1, devices, end, 0)


def route(buffer, counts, devices, seq_count):
    capacity, width = buffer.shape[1:]
    lanes = counts.shape[2]
    return pl.pallas_call(
        functools.partial(route_kernel, devices, seq_count),
        in_specs=[pl.BlockSpec(memory_space=pl.ANY)] * 2,
        out_specs=[pl.BlockSpec(memory_space=pl.ANY)] * 2,
        out_shape=(
            jax.ShapeDtypeStruct((devices, capacity, width), BF16),
            jax.ShapeDtypeStruct((devices, 1, lanes), jnp.int32),
        ),
        scratch_shapes=[pltpu.SemaphoreType.DMA((devices,))] * 4
        + [pltpu.SemaphoreType.DMA((2,))],
        compiler_params=pltpu.CompilerParams(collective_id=1, has_side_effects=True),
        name="route",
    )(buffer, counts)


def write_masks(capacity, seq_count, counts_ref, bias_ref, mask_ref):
    devices, lanes = counts_ref.shape
    slots = mask_ref.shape[0]
    half, quarter = slots // 2, slots // 4
    slide = lax.axis_index("slide")
    seq = lax.axis_index("seq")
    core = lax.rem(seq, 2)
    chip = lax.rem(seq // 2, 2)
    base = slide * seq_count + seq - core - 2 * chip
    members = [
        base + core + 2 * chip,
        base + (1 - core) + 2 * chip,
        base + core + 2 * (1 - chip),
        base + (1 - core) + 2 * (1 - chip),
    ]
    counts = counts_ref[...].astype(F32)
    lane = lax.broadcasted_iota(jnp.int32, (devices, lanes), 1)
    columns = [
        jnp.sum(jnp.where(lane == member, counts, 0.0), axis=1, keepdims=True)
        for member in members
    ]
    sender = lax.broadcasted_iota(jnp.int32, (devices, slots), 0) * capacity
    index = lax.broadcasted_iota(jnp.int32, (devices, slots), 1)

    def row(position, reached):
        place = (position - sender).astype(F32)
        inside = jnp.logical_and(place >= 0.0, place < reached)
        return (jnp.sum(inside.astype(F32), axis=0, keepdims=True) - 1.0) * (-MASKED)

    bias_ref[0:1, :] = row(original_of(index, quarter), columns[0])
    within = jnp.where(index >= half, index - half, index)
    for parity in range(2):
        reached = jnp.where(index >= half, columns[1], columns[0])
        bias_ref[1 + parity : 2 + parity, :] = row(
            original_of(within + parity * half, quarter), reached
        )
    for phase in range(4):
        block = (
            (index >= quarter).astype(jnp.int32)
            + (index >= 2 * quarter).astype(jnp.int32)
            + (index >= 3 * quarter).astype(jnp.int32)
        )
        reached = jnp.where(
            index >= half,
            jnp.where(index >= 3 * quarter, columns[3], columns[2]),
            jnp.where(index >= quarter, columns[1], columns[0]),
        )
        bias_ref[3 + phase : 4 + phase, :] = row(4 * (index - quarter * block) + phase, reached)
    bias_ref[7:8, :] = jnp.zeros((1, slots), F32)
    own = (lax.broadcasted_iota(jnp.int32, (8, lanes), 1) == members[0]).astype(F32)
    reached = lax.dot_general(
        own, counts, (((1,), (1,)), ((), ())), preferred_element_type=F32
    )[0:1, :]
    place = (
        lax.broadcasted_iota(jnp.int32, (slots, devices), 0)
        - lax.broadcasted_iota(jnp.int32, (slots, devices), 1) * capacity
    ).astype(F32)
    inside = jnp.logical_and(place >= 0.0, place < reached)
    mask_ref[...] = (jnp.sum(inside.astype(F32), axis=1, keepdims=True) - 1.0) * (-MASKED)


def project_kernel(capacity, seq_count, tiles_ref, gain_ref, counts_ref, weight_ref, out_ref, near_ref, far_ref, normed_ref, bias_ref, mask_ref):
    step = pl.program_id(0)
    slots, width = tiles_ref.shape
    quarter = slots // 4
    half = slots // 2

    @pl.when(step == 0)
    def _():
        tile = tiles_ref[...].astype(F32)
        mean = jnp.mean(tile * tile, axis=1, keepdims=True)
        normed = (tile * lax.rsqrt(mean + EPSILON) * gain_ref[...]).astype(BF16)
        index = lax.broadcasted_iota(jnp.int32, (slots, slots), 0)
        position = lax.broadcasted_iota(jnp.int32, (slots, slots), 1)
        order = (original_of(index, quarter) == position).astype(F32).astype(BF16)
        for start in range(0, width, WIDE):
            normed_ref[:, start : start + WIDE] = jnp.dot(
                order, normed[:, start : start + WIDE], preferred_element_type=F32
            ).astype(BF16)
        write_masks(capacity, seq_count, counts_ref, bias_ref, mask_ref)

    value = jnp.dot(normed_ref[...], weight_ref[...], preferred_element_type=F32).astype(BF16)
    out_ref[...] = value
    for j in range(GROUP):
        cols = slice(j * HEAD, (j + 1) * HEAD)
        near_ref[:, cols] = value[(j % 2) * half : (j % 2 + 1) * half, cols]
        begin = QUARTER_OF[j] * quarter
        far_ref[:, cols] = value[begin : begin + quarter, cols]


def project(tiles, gain, counts, weight, capacity, seq_count):
    slots, width = tiles.shape
    steps = width // WIDE
    whole = lambda i: (0, 0)
    return pl.pallas_call(
        functools.partial(project_kernel, capacity, seq_count),
        grid=(2 * steps,),
        in_specs=[
            pl.BlockSpec((slots, width), whole),
            pl.BlockSpec((1, width), whole),
            pl.BlockSpec(counts.shape, whole),
            pl.BlockSpec((width, WIDE), lambda i: (0, i + steps)),
        ],
        out_specs=[
            pl.BlockSpec((slots, WIDE), lambda i: (0, i)),
            pl.BlockSpec((slots // 2, WIDE), lambda i: (0, i)),
            pl.BlockSpec((slots // 4, WIDE), lambda i: (0, i)),
            pl.BlockSpec((slots, width), whole),
            pl.BlockSpec((8, slots), whole),
            pl.BlockSpec((slots, 1), whole),
        ],
        out_shape=(
            jax.ShapeDtypeStruct((slots, 2 * width), BF16),
            jax.ShapeDtypeStruct((slots // 2, 2 * width), BF16),
            jax.ShapeDtypeStruct((slots // 4, 2 * width), BF16),
            jax.ShapeDtypeStruct((slots, width), BF16),
            jax.ShapeDtypeStruct((8, slots), F32),
            jax.ShapeDtypeStruct((slots, 1), F32),
        ),
        compiler_params=params(),
        name="project",
    )(tiles, gain.reshape(1, width), counts, weight)


def query_kernel(normed_ref, weight_ref, out_ref):
    out_ref[...] = jnp.dot(
        normed_ref[...], weight_ref[...], preferred_element_type=F32
    ).astype(BF16)


def project_query(normed, weight):
    slots, width = normed.shape
    return pl.pallas_call(
        query_kernel,
        grid=(width // WIDE,),
        in_specs=[
            pl.BlockSpec((slots, width), lambda i: (0, 0)),
            pl.BlockSpec((width, WIDE), lambda i: (0, i)),
        ],
        out_specs=pl.BlockSpec((slots, WIDE), lambda i: (0, i)),
        out_shape=jax.ShapeDtypeStruct((slots, width), BF16),
        compiler_params=params(),
        cost_estimate=pl.CostEstimate(
            flops=2 * slots * width * width, bytes_accessed=10_000_000, transcendentals=0
        ),
        name="project_query",
    )(normed, weight)


def softmax_parts(query, keys, values, bias):
    scores = lax.dot_general(
        query, keys, (((1,), (1,)), ((), ())), preferred_element_type=F32
    )
    scores = scores * FACTOR + bias
    peak = jnp.max(scores, axis=1, keepdims=True)
    weights = jnp.exp2(scores - peak)
    total = jnp.sum(weights, axis=1, keepdims=True)
    summed = jnp.dot(weights.astype(BF16), values, preferred_element_type=F32)
    return summed, peak, total


def merge(parts):
    top = parts[0][1]
    for _, peak, _ in parts[1:]:
        top = jnp.maximum(top, peak)
    above, below = 0.0, 0.0
    for summed, peak, total in parts:
        factor = jnp.exp2(peak - top)
        above = above + factor * summed
        below = below + factor * total
    return above, top, below


def ratio(above, below):
    return (above * (1.0 / jnp.maximum(below, 1.0))).astype(BF16)


def near_attention_kernel(
    q_ref, k_ref, v_ref, bias_ref, pair_k, pair_v, mixed_ref, summed_ref, stats_ref
):
    slots = q_ref.shape[0]
    half, quarter = slots // 2, slots // 4
    lanes = lax.broadcasted_iota(jnp.int32, (quarter, HEAD), 1)
    stats = jnp.zeros((quarter, HEAD), F32)
    for j in range(GROUP):
        cols = slice(j * HEAD, (j + 1) * HEAD)
        start = (j % 2) * half
        inside = QUARTER_OF[j] * quarter - start
        mine = slice(start, start + half)
        other = slice(half - start, 2 * half - start)
        summed, _, total = softmax_parts(
            q_ref[other, cols], k_ref[:, cols], v_ref[:, cols], bias_ref[0:1, :]
        )
        mixed_ref[other, cols] = ratio(summed, total)
        one = softmax_parts(q_ref[mine, cols], k_ref[:, cols], v_ref[:, cols], bias_ref[0:1, :])
        keys = jnp.concatenate([k_ref[mine, cols], pair_k[:, cols]], axis=0)
        values = jnp.concatenate([v_ref[mine, cols], pair_v[:, cols]], axis=0)
        two = softmax_parts(q_ref[mine, cols], keys, values, bias_ref[1 + j % 2 : 2 + j % 2, :])
        above, top, below = merge([one, two])
        done = quarter - inside
        mixed_ref[start + done : start + done + quarter, cols] = ratio(
            above[done : done + quarter], below[done : done + quarter]
        )
        summed_ref[:, cols] = above[inside : inside + quarter]
        stats = jnp.where(
            lanes == 2 * j,
            top[inside : inside + quarter],
            jnp.where(lanes == 2 * j + 1, below[inside : inside + quarter], stats),
        )
        begin = start + inside
        mixed_ref[begin : begin + quarter, cols] = jnp.zeros((quarter, HEAD), BF16)
    stats_ref[...] = stats


def halves(array, steps):
    rows = array.shape[0]
    return [
        pl.BlockSpec((rows, WIDE), lambda i: (0, i)),
        pl.BlockSpec((rows, WIDE), lambda i: (0, i + steps)),
    ]


def near_attention(query, pairs, bias, pair):
    slots, width = query.shape
    quarter = slots // 4
    steps = width // WIDE
    return pl.pallas_call(
        near_attention_kernel,
        grid=(steps,),
        in_specs=[
            pl.BlockSpec((slots, WIDE), lambda i: (0, i)),
            *halves(pairs, steps),
            pl.BlockSpec(bias.shape, lambda i: (0, 0)),
            *halves(pair, steps),
        ],
        out_specs=[
            pl.BlockSpec((slots, WIDE), lambda i: (0, i)),
            pl.BlockSpec((quarter, WIDE), lambda i: (0, i)),
            pl.BlockSpec((quarter, HEAD), lambda i: (0, i)),
        ],
        out_shape=(
            jax.ShapeDtypeStruct((slots, width), BF16),
            jax.ShapeDtypeStruct((quarter, width), F32),
            jax.ShapeDtypeStruct((quarter, steps * HEAD), F32),
        ),
        compiler_params=params(),
        cost_estimate=pl.CostEstimate(
            flops=12 * slots * slots * width,
            bytes_accessed=14_000_000,
            transcendentals=6 * slots * slots * HEADS,
        ),
        name="near_attention",
    )(query, pairs, pairs, bias, pair, pair)


def far_attention_kernel(
    q_ref, k_ref, v_ref, bias_ref, pair_k, pair_v, one_k, one_v, two_k, two_v,
    summed_ref, stats_ref, near_ref, mixed_ref,
):
    slots = q_ref.shape[0]
    half, quarter = slots // 2, slots // 4
    mixed_ref[...] = near_ref[...]
    for j in range(GROUP):
        cols = slice(j * HEAD, (j + 1) * HEAD)
        begin = QUARTER_OF[j] * quarter
        inside = begin - (j % 2) * half
        fourth = slice(begin, begin + quarter)
        within = slice(inside, inside + quarter)
        keys = jnp.concatenate(
            [k_ref[fourth, cols], pair_k[within, cols], one_k[:, cols], two_k[:, cols]], axis=0
        )
        values = jnp.concatenate(
            [v_ref[fourth, cols], pair_v[within, cols], one_v[:, cols], two_v[:, cols]], axis=0
        )
        four = softmax_parts(q_ref[fourth, cols], keys, values, bias_ref[3 + j : 4 + j, :])
        before = (
            summed_ref[:, cols],
            stats_ref[:, 2 * j : 2 * j + 1],
            stats_ref[:, 2 * j + 1 : 2 * j + 2],
        )
        above, _, below = merge([before, four])
        mixed_ref[fourth, cols] = ratio(above, below)


def far_attention(query, pairs, bias, pair, one, two, mixed, summed, stats):
    slots, width = query.shape
    quarter = slots // 4
    steps = width // WIDE
    block = pl.BlockSpec((slots, WIDE), lambda i: (0, i))
    return pl.pallas_call(
        far_attention_kernel,
        grid=(steps,),
        in_specs=[
            block,
            *halves(pairs, steps),
            pl.BlockSpec(bias.shape, lambda i: (0, 0)),
            *halves(pair, steps),
            *halves(one, steps),
            *halves(two, steps),
            pl.BlockSpec((quarter, WIDE), lambda i: (0, i)),
            pl.BlockSpec((quarter, HEAD), lambda i: (0, i)),
            block,
        ],
        out_specs=block,
        out_shape=jax.ShapeDtypeStruct((slots, width), BF16),
        compiler_params=params(),
        name="far_attention",
    )(query, pairs, pairs, bias, pair, pair, one, one, two, two, summed, stats, mixed)


def finish_kernel(mixed_ref, tiles_ref, weight_ref, finding_ref, mask_ref, layer_ref, keys_ref, stats_ref, plain_ref):
    slots, width = tiles_ref.shape
    quarter = slots // 4
    position = lax.broadcasted_iota(jnp.int32, (slots, slots), 0)
    index = lax.broadcasted_iota(jnp.int32, (slots, slots), 1)
    order = (original_of(index, quarter) == position).astype(F32).astype(BF16)
    for start in range(0, width, WIDE):
        plain_ref[:, start : start + WIDE] = jnp.dot(
            order, mixed_ref[:, start : start + WIDE], preferred_element_type=F32
        ).astype(BF16)
    square = jnp.zeros((slots, 1), F32)
    for start in range(0, width, WIDE):
        cols = slice(start, start + WIDE)
        added = jnp.dot(plain_ref[...], weight_ref[:, cols], preferred_element_type=F32)
        out = (tiles_ref[:, cols].astype(F32) + added).astype(BF16)
        layer_ref[:, cols] = out
        wide = out.astype(F32)
        square = square + jnp.sum(wide * wide, axis=1, keepdims=True)
    inverse = lax.rsqrt(square * (1.0 / width) + EPSILON)
    mask = mask_ref[...]
    for h in range(HEADS):
        cols = slice(h * HEAD, (h + 1) * HEAD)
        keys = (layer_ref[:, cols].astype(F32) * inverse).astype(BF16)
        keys_ref[:, cols] = keys
        scores = lax.dot_general(
            keys, finding_ref[:, cols], (((1,), (1,)), ((), ())), preferred_element_type=F32
        )
        scores = scores * FACTOR + mask
        peak = jnp.max(scores, axis=0, keepdims=True)
        stats_ref[h : h + 1, :] = peak
        stats_ref[HEADS + h : HEADS + h + 1, :] = jnp.sum(
            jnp.exp2(scores - peak), axis=0, keepdims=True
        )


def finish(mixed, tiles, weight, finding, mask):
    slots, width = tiles.shape
    return pl.pallas_call(
        finish_kernel,
        out_shape=(
            jax.ShapeDtypeStruct((slots, width), BF16),
            jax.ShapeDtypeStruct((slots, width), BF16),
            jax.ShapeDtypeStruct((2 * HEADS, finding.shape[0]), F32),
        ),
        scratch_shapes=[pltpu.VMEM((slots, width), BF16)],
        compiler_params=params(),
        name="finish",
    )(mixed, tiles, weight, finding, mask)


def heat_kernel(count, scale, stats_ref, keys_ref, finding_ref, mask_ref, heat_ref, held, send_sem, recv_sem):
    slide = lax.axis_index("slide")
    me = lax.axis_index("seq")
    barrier = pltpu.get_barrier_semaphore()
    for hop in range(1, count):
        peer = lax.rem(me + hop, count)
        pl.semaphore_signal(
            barrier, inc=1, device_id=(slide, peer), device_id_type=pl.DeviceIdType.MESH
        )
    pl.semaphore_wait(barrier, count - 1)
    copies = []
    for hop in range(1, count):
        peer = lax.rem(me + hop, count)
        copy = pltpu.make_async_remote_copy(
            src_ref=stats_ref,
            dst_ref=held.at[hop],
            send_sem=send_sem.at[hop],
            recv_sem=recv_sem.at[hop],
            device_id=(slide, peer),
            device_id_type=pl.DeviceIdType.MESH,
        )
        copy.start()
        copies.append(copy)
    for copy in copies:
        copy.wait()
    everything = [stats_ref[...]] + [held[hop] for hop in range(1, count)]
    peaks = everything[0][:HEADS]
    for part in everything[1:]:
        peaks = jnp.maximum(peaks, part[:HEADS])
    totals = jnp.zeros_like(peaks)
    for part in everything:
        totals = totals + part[HEADS:] * jnp.exp2(part[:HEADS] - peaks)
    factors = scale / totals
    slots = keys_ref.shape[0]
    chunk = slots // 2
    for start in range(0, slots, chunk):
        rows = slice(start, start + chunk)
        mask = mask_ref[rows, :]
        total = jnp.zeros((chunk, finding_ref.shape[0]), F32)
        for h in range(HEADS):
            cols = slice(h * HEAD, (h + 1) * HEAD)
            scores = lax.dot_general(
                keys_ref[rows, cols], finding_ref[:, cols], (((1,), (1,)), ((), ())),
                preferred_element_type=F32,
            )
            scores = scores * FACTOR + mask
            total = total + jnp.exp2(scores - peaks[h : h + 1]) * factors[h : h + 1]
        heat_ref[rows, :] = total


def heat_map(count, stats, keys, finding, mask):
    slots = keys.shape[0]
    finds = finding.shape[0]
    return pl.pallas_call(
        functools.partial(heat_kernel, count, count * slots / HEADS),
        in_specs=[pl.BlockSpec(memory_space=pltpu.VMEM)] * 4,
        out_specs=pl.BlockSpec(memory_space=pltpu.VMEM),
        out_shape=jax.ShapeDtypeStruct((slots, finds), F32),
        scratch_shapes=[
            pltpu.VMEM((count, 2 * HEADS, finds), F32),
            pltpu.SemaphoreType.DMA((count,)),
            pltpu.SemaphoreType.DMA((count,)),
        ],
        compiler_params=params(collective_id=0, has_side_effects=True),
        name="heat_map",
    )(stats, keys, finding, mask)


def exchange(value, mask):
    pairs = [(source, source ^ mask) for source in range(lax.axis_size("seq"))]
    return lax.ppermute(value, "seq", pairs)


def shards(embeds, destination, norm_gain, qkv_weight, out_weight, finding_queries):
    devices = lax.axis_size(("slide", "seq"))
    seq_count = lax.axis_size("seq")
    slots = embeds.shape[0] * 2
    capacity = slots // devices
    padded = -(-capacity // 8) * 8
    width = embeds.shape[1]
    buffer, counts = dispatch(destination, embeds, devices, padded)
    received, counts = route(
        buffer.reshape(devices, padded, width), counts[None], devices, seq_count
    )
    tiles = received[:, :capacity].reshape(slots, width)
    pairs, near, far, normed, bias, mask = project(
        tiles, norm_gain, counts[:, 0], qkv_weight, capacity, seq_count
    )
    one = exchange(far, 2)
    pair = exchange(near, 1)
    query = project_query(normed, qkv_weight)
    mixed, summed, stats = near_attention(query, pairs, bias, pair)
    one, mixed = lax.optimization_barrier((one, mixed))
    two = exchange(one, 1)
    mixed = far_attention(query, pairs, bias, pair, one, two, mixed, summed, stats)
    layer_out, keys, stats = finish(mixed, tiles, out_weight, finding_queries, mask)
    heat = heat_map(seq_count, stats, keys, finding_queries, mask)
    return (layer_out, heat)


def solution(mesh):
    in_specs = (P(("slide", "seq"), None), P(("slide", "seq"), None), P(), P(), P(), P())
    out_specs = (P(("slide", "seq"), None), P(("slide", "seq"), None))
    return jax.shard_map(shards, mesh=mesh, in_specs=in_specs, out_specs=out_specs, check_vma=False)
```

```python
import functools
import math

import jax
import jax.numpy as jnp
from jax import lax
from jax.experimental import pallas as pl
from jax.experimental.pallas import tpu as pltpu
from jax.sharding import PartitionSpec as P

HEADS = 12
HEAD = 128
GROUP = 4
WIDE = GROUP * HEAD
MASKED = -1e30
EPSILON = 1e-06
FACTOR = math.log2(math.e) / math.sqrt(HEAD)
F32 = jnp.float32
BF16 = jnp.bfloat16
QUARTER_OF = (0, 2, 1, 3)
VMEM_LIMIT = 56 * 1024 * 1024
SMALL_LIMIT = 34 * 1024 * 1024


def params(limit=VMEM_LIMIT, **more):
    return pltpu.CompilerParams(vmem_limit_bytes=limit, **more)


def dispatch_kernel(capacity, row_ref, embeds_ref, buffer_ref, counts_ref):
    rows = embeds_ref.shape[0]
    slots = buffer_ref.shape[0]
    row = row_ref[...]
    col = jnp.transpose(jnp.broadcast_to(row.astype(F32), (128, rows)))[:, 0:1].astype(jnp.int32)
    first = lax.broadcasted_iota(jnp.int32, (rows, rows), 0)
    second = lax.broadcasted_iota(jnp.int32, (rows, rows), 1)
    same = jnp.logical_and(col == row, first < second)
    rank = jnp.sum(same.astype(F32), axis=0, keepdims=True).astype(jnp.int32)
    place = row * capacity + rank
    lanes = lax.broadcasted_iota(jnp.int32, (rows, counts_ref.shape[1]), 1)
    counts_ref[...] = jnp.sum((col == lanes).astype(F32), axis=0, keepdims=True).astype(jnp.int32)
    chosen = (lax.broadcasted_iota(jnp.int32, (slots, rows), 0) == place).astype(F32).astype(BF16)
    for start in range(0, embeds_ref.shape[1], WIDE):
        part = embeds_ref[:, start : start + WIDE]
        buffer_ref[:, start : start + WIDE] = jnp.dot(
            chosen, part, preferred_element_type=F32
        ).astype(BF16)


def dispatch(destination, embeds, devices, capacity):
    rows, width = embeds.shape
    slots = devices * capacity
    return pl.pallas_call(
        functools.partial(dispatch_kernel, capacity),
        out_shape=(
            jax.ShapeDtypeStruct((slots, width), BF16),
            jax.ShapeDtypeStruct((1, max(128, devices)), jnp.int32),
        ),
        compiler_params=params(),
        name="dispatch",
    )(destination.reshape(1, rows), embeds)


def original_of(index, quarter):
    block = (
        (index >= quarter).astype(jnp.int32)
        + (index >= 2 * quarter).astype(jnp.int32)
        + (index >= 3 * quarter).astype(jnp.int32)
    )
    phase = 2 * jnp.where((block == 1) | (block == 3), 1, 0) + (block >= 2).astype(jnp.int32)
    return 4 * (index - quarter * block) + phase


def route_kernel(devices, seq_count, buffer_ref, counts_ref, tiles_ref, all_ref, send, recv, count_send, count_recv, own_sem):
    me = lax.axis_index("slide") * seq_count + lax.axis_index("seq")
    barrier = pltpu.get_barrier_semaphore()

    def place_of(hop):
        peer = lax.rem(me + hop, devices)
        return peer, (peer // seq_count, lax.rem(peer, seq_count))

    def greet(hop, carry):
        pl.semaphore_signal(
            barrier, inc=1, device_id=place_of(hop)[1], device_id_type=pl.DeviceIdType.MESH
        )
        return carry

    lax.fori_loop(1, devices, greet, 0)
    pl.semaphore_wait(barrier, devices - 1)

    def copies(hop):
        peer, where = place_of(hop)
        rows = pltpu.make_async_remote_copy(
            src_ref=buffer_ref.at[peer],
            dst_ref=tiles_ref.at[me],
            send_sem=send.at[hop],
            recv_sem=recv.at[hop],
            device_id=where,
            device_id_type=pl.DeviceIdType.MESH,
        )
        count = pltpu.make_async_remote_copy(
            src_ref=counts_ref.at[0],
            dst_ref=all_ref.at[me],
            send_sem=count_send.at[hop],
            recv_sem=count_recv.at[hop],
            device_id=where,
            device_id_type=pl.DeviceIdType.MESH,
        )
        return rows, count

    def begin(hop, carry):
        for copy in copies(hop):
            copy.start()
        return carry

    def end(hop, carry):
        for copy in copies(hop):
            copy.wait()
        return carry

    own_rows = pltpu.make_async_copy(buffer_ref.at[me], tiles_ref.at[me], own_sem.at[0])
    own_count = pltpu.make_async_copy(counts_ref.at[0], all_ref.at[me], own_sem.at[1])
    lax.fori_loop(1, devices, begin, 0)
    own_rows.start()
    own_count.start()
    own_rows.wait()
    own_count.wait()
    lax.fori_loop(1, devices, end, 0)


def route(buffer, counts, devices, seq_count):
    capacity, width = buffer.shape[1:]
    lanes = counts.shape[2]
    return pl.pallas_call(
        functools.partial(route_kernel, devices, seq_count),
        in_specs=[pl.BlockSpec(memory_space=pl.ANY)] * 2,
        out_specs=[pl.BlockSpec(memory_space=pl.ANY)] * 2,
        out_shape=(
            jax.ShapeDtypeStruct((devices, capacity, width), BF16),
            jax.ShapeDtypeStruct((devices, 1, lanes), jnp.int32),
        ),
        scratch_shapes=[pltpu.SemaphoreType.DMA((devices,))] * 4
        + [pltpu.SemaphoreType.DMA((2,))],
        compiler_params=pltpu.CompilerParams(collective_id=1, has_side_effects=True),
        name="route",
    )(buffer, counts)


def write_masks(capacity, seq_count, counts_ref, bias_ref, mask_ref):
    devices, lanes = counts_ref.shape
    slots = mask_ref.shape[0]
    half, quarter = slots // 2, slots // 4
    slide = lax.axis_index("slide")
    seq = lax.axis_index("seq")
    core = lax.rem(seq, 2)
    chip = lax.rem(seq // 2, 2)
    base = slide * seq_count + seq - core - 2 * chip
    members = [
        base + core + 2 * chip,
        base + (1 - core) + 2 * chip,
        base + core + 2 * (1 - chip),
        base + (1 - core) + 2 * (1 - chip),
    ]
    counts = counts_ref[...].astype(F32)
    lane = lax.broadcasted_iota(jnp.int32, (devices, lanes), 1)
    columns = [
        jnp.sum(jnp.where(lane == member, counts, 0.0), axis=1, keepdims=True)
        for member in members
    ]
    sender = lax.broadcasted_iota(jnp.int32, (devices, slots), 0) * capacity
    index = lax.broadcasted_iota(jnp.int32, (devices, slots), 1)

    def row(position, reached):
        place = (position - sender).astype(F32)
        inside = jnp.logical_and(place >= 0.0, place < reached)
        return (jnp.sum(inside.astype(F32), axis=0, keepdims=True) - 1.0) * (-MASKED)

    bias_ref[0:1, :] = row(original_of(index, quarter), columns[0])
    within = jnp.where(index >= half, index - half, index)
    for parity in range(2):
        reached = jnp.where(index >= half, columns[1], columns[0])
        bias_ref[1 + parity : 2 + parity, :] = row(
            original_of(within + parity * half, quarter), reached
        )
    for phase in range(4):
        block = (
            (index >= quarter).astype(jnp.int32)
            + (index >= 2 * quarter).astype(jnp.int32)
            + (index >= 3 * quarter).astype(jnp.int32)
        )
        reached = jnp.where(
            index >= half,
            jnp.where(index >= 3 * quarter, columns[3], columns[2]),
            jnp.where(index >= quarter, columns[1], columns[0]),
        )
        bias_ref[3 + phase : 4 + phase, :] = row(4 * (index - quarter * block) + phase, reached)
    bias_ref[7:8, :] = jnp.zeros((1, slots), F32)
    own = (lax.broadcasted_iota(jnp.int32, (8, lanes), 1) == members[0]).astype(F32)
    reached = lax.dot_general(
        own, counts, (((1,), (1,)), ((), ())), preferred_element_type=F32
    )[0:1, :]
    place = (
        lax.broadcasted_iota(jnp.int32, (slots, devices), 0)
        - lax.broadcasted_iota(jnp.int32, (slots, devices), 1) * capacity
    ).astype(F32)
    inside = jnp.logical_and(place >= 0.0, place < reached)
    mask_ref[...] = (jnp.sum(inside.astype(F32), axis=1, keepdims=True) - 1.0) * (-MASKED)


def project_kernel(capacity, seq_count, tiles_ref, gain_ref, counts_ref, weight_ref, out_ref, near_ref, far_ref, normed_ref, bias_ref, mask_ref):
    step = pl.program_id(0)
    slots, width = tiles_ref.shape
    quarter = slots // 4
    half = slots // 2

    @pl.when(step == 0)
    def _():
        tile = tiles_ref[...].astype(F32)
        mean = jnp.mean(tile * tile, axis=1, keepdims=True)
        normed = (tile * lax.rsqrt(mean + EPSILON) * gain_ref[...]).astype(BF16)
        index = lax.broadcasted_iota(jnp.int32, (slots, slots), 0)
        position = lax.broadcasted_iota(jnp.int32, (slots, slots), 1)
        order = (original_of(index, quarter) == position).astype(F32).astype(BF16)
        for start in range(0, width, WIDE):
            normed_ref[:, start : start + WIDE] = jnp.dot(
                order, normed[:, start : start + WIDE], preferred_element_type=F32
            ).astype(BF16)
        write_masks(capacity, seq_count, counts_ref, bias_ref, mask_ref)

    value = jnp.dot(normed_ref[...], weight_ref[...], preferred_element_type=F32).astype(BF16)
    out_ref[...] = value
    for j in range(GROUP):
        cols = slice(j * HEAD, (j + 1) * HEAD)
        near_ref[:, cols] = value[(j % 2) * half : (j % 2 + 1) * half, cols]
        begin = QUARTER_OF[j] * quarter
        far_ref[:, cols] = value[begin : begin + quarter, cols]


def project(tiles, gain, counts, weight, capacity, seq_count):
    slots, width = tiles.shape
    steps = width // WIDE
    whole = lambda i: (0, 0)
    return pl.pallas_call(
        functools.partial(project_kernel, capacity, seq_count),
        grid=(2 * steps,),
        in_specs=[
            pl.BlockSpec((slots, width), whole),
            pl.BlockSpec((1, width), whole),
            pl.BlockSpec(counts.shape, whole),
            pl.BlockSpec((width, WIDE), lambda i: (0, i + steps)),
        ],
        out_specs=[
            pl.BlockSpec((slots, WIDE), lambda i: (0, i)),
            pl.BlockSpec((slots // 2, WIDE), lambda i: (0, i)),
            pl.BlockSpec((slots // 4, WIDE), lambda i: (0, i)),
            pl.BlockSpec((slots, width), whole),
            pl.BlockSpec((8, slots), whole),
            pl.BlockSpec((slots, 1), whole),
        ],
        out_shape=(
            jax.ShapeDtypeStruct((slots, 2 * width), BF16),
            jax.ShapeDtypeStruct((slots // 2, 2 * width), BF16),
            jax.ShapeDtypeStruct((slots // 4, 2 * width), BF16),
            jax.ShapeDtypeStruct((slots, width), BF16),
            jax.ShapeDtypeStruct((8, slots), F32),
            jax.ShapeDtypeStruct((slots, 1), F32),
        ),
        compiler_params=params(),
        name="project",
    )(tiles, gain.reshape(1, width), counts, weight)


def query_kernel(normed_ref, weight_ref, out_ref):
    out_ref[...] = jnp.dot(
        normed_ref[...], weight_ref[...], preferred_element_type=F32
    ).astype(BF16)


def project_query(normed, weight):
    slots, width = normed.shape
    return pl.pallas_call(
        query_kernel,
        grid=(width // WIDE,),
        in_specs=[
            pl.BlockSpec((slots, width), lambda i: (0, 0)),
            pl.BlockSpec((width, WIDE), lambda i: (0, i)),
        ],
        out_specs=pl.BlockSpec((slots, WIDE), lambda i: (0, i)),
        out_shape=jax.ShapeDtypeStruct((slots, width), BF16),
        compiler_params=params(),
        cost_estimate=pl.CostEstimate(
            flops=2 * slots * width * width, bytes_accessed=10_000_000, transcendentals=0
        ),
        name="project_query",
    )(normed, weight)


def softmax_parts(query, keys, values, bias):
    scores = lax.dot_general(
        query, keys, (((1,), (1,)), ((), ())), preferred_element_type=F32
    )
    scores = scores * FACTOR + bias
    peak = jnp.max(scores, axis=1, keepdims=True)
    weights = jnp.exp2(scores - peak)
    total = jnp.sum(weights, axis=1, keepdims=True)
    summed = jnp.dot(weights.astype(BF16), values, preferred_element_type=F32)
    return summed, peak, total


def merge(parts):
    top = parts[0][1]
    for _, peak, _ in parts[1:]:
        top = jnp.maximum(top, peak)
    above, below = 0.0, 0.0
    for summed, peak, total in parts:
        factor = jnp.exp2(peak - top)
        above = above + factor * summed
        below = below + factor * total
    return above, top, below


def ratio(above, below):
    return (above * (1.0 / jnp.maximum(below, 1.0))).astype(BF16)


def near_attention_kernel(
    q_ref, k_ref, v_ref, bias_ref, pair_k, pair_v, mixed_ref, summed_ref, stats_ref, query_ref
):
    slots = q_ref.shape[0]
    half, quarter = slots // 2, slots // 4
    lanes = lax.broadcasted_iota(jnp.int32, (quarter, HEAD), 1)
    stats = jnp.zeros((quarter, HEAD), F32)
    for j in range(GROUP):
        cols = slice(j * HEAD, (j + 1) * HEAD)
        start = (j % 2) * half
        inside = QUARTER_OF[j] * quarter - start
        mine = slice(start, start + half)
        other = slice(half - start, 2 * half - start)
        summed, _, total = softmax_parts(
            q_ref[other, cols], k_ref[:, cols], v_ref[:, cols], bias_ref[0:1, :]
        )
        mixed_ref[other, cols] = ratio(summed, total)
        one = softmax_parts(q_ref[mine, cols], k_ref[:, cols], v_ref[:, cols], bias_ref[0:1, :])
        keys = jnp.concatenate([k_ref[mine, cols], pair_k[:, cols]], axis=0)
        values = jnp.concatenate([v_ref[mine, cols], pair_v[:, cols]], axis=0)
        two = softmax_parts(q_ref[mine, cols], keys, values, bias_ref[1 + j % 2 : 2 + j % 2, :])
        above, top, below = merge([one, two])
        done = quarter - inside
        mixed_ref[start + done : start + done + quarter, cols] = ratio(
            above[done : done + quarter], below[done : done + quarter]
        )
        begin = start + inside
        fourth = slice(begin, begin + quarter)
        within = slice(inside, inside + quarter)
        keys = jnp.concatenate([k_ref[fourth, cols], pair_k[within, cols]], axis=0)
        values = jnp.concatenate([v_ref[fourth, cols], pair_v[within, cols]], axis=0)
        four = softmax_parts(q_ref[fourth, cols], keys, values, bias_ref[3 + j : 4 + j, :half])
        above, top, below = merge([(above[within], top[within], below[within]), four])
        summed_ref[:, cols] = above
        stats = jnp.where(lanes == 2 * j, top, jnp.where(lanes == 2 * j + 1, below, stats))
        query_ref[:, cols] = q_ref[fourth, cols]
        mixed_ref[fourth, cols] = jnp.zeros((quarter, HEAD), BF16)
    stats_ref[...] = stats


def halves(array, steps):
    rows = array.shape[0]
    return [
        pl.BlockSpec((rows, WIDE), lambda i: (0, i)),
        pl.BlockSpec((rows, WIDE), lambda i: (0, i + steps)),
    ]


def near_attention(query, pairs, bias, pair):
    slots, width = query.shape
    quarter = slots // 4
    steps = width // WIDE
    return pl.pallas_call(
        near_attention_kernel,
        grid=(steps,),
        in_specs=[
            pl.BlockSpec((slots, WIDE), lambda i: (0, i)),
            *halves(pairs, steps),
            pl.BlockSpec(bias.shape, lambda i: (0, 0)),
            *halves(pair, steps),
        ],
        out_specs=[
            pl.BlockSpec((slots, WIDE), lambda i: (0, i)),
            pl.BlockSpec((quarter, WIDE), lambda i: (0, i)),
            pl.BlockSpec((quarter, HEAD), lambda i: (0, i)),
            pl.BlockSpec((quarter, WIDE), lambda i: (0, i)),
        ],
        out_shape=(
            jax.ShapeDtypeStruct((slots, width), BF16),
            jax.ShapeDtypeStruct((quarter, width), F32),
            jax.ShapeDtypeStruct((quarter, steps * HEAD), F32),
            jax.ShapeDtypeStruct((quarter, width), BF16),
        ),
        compiler_params=params(SMALL_LIMIT),
        cost_estimate=pl.CostEstimate(
            flops=12 * slots * slots * width,
            bytes_accessed=14_000_000,
            transcendentals=6 * slots * slots * HEADS,
        ),
        name="near_attention",
    )(query, pairs, pairs, bias, pair, pair)


def far_attention_kernel(
    q_ref, bias_ref, one_k, one_v, two_k, two_v, summed_ref, stats_ref, mixed_ref
):
    half = bias_ref.shape[1] // 2
    for j in range(GROUP):
        cols = slice(j * HEAD, (j + 1) * HEAD)
        keys = jnp.concatenate([one_k[:, cols], two_k[:, cols]], axis=0)
        values = jnp.concatenate([one_v[:, cols], two_v[:, cols]], axis=0)
        four = softmax_parts(q_ref[:, cols], keys, values, bias_ref[3 + j : 4 + j, half:])
        before = (
            summed_ref[:, cols],
            stats_ref[:, 2 * j : 2 * j + 1],
            stats_ref[:, 2 * j + 1 : 2 * j + 2],
        )
        above, _, below = merge([before, four])
        mixed_ref[:, cols] = ratio(above, below)


def far_attention(query, bias, one, two, summed, stats):
    quarter, width = query.shape
    steps = width // WIDE
    block = pl.BlockSpec((quarter, WIDE), lambda i: (0, i))
    return pl.pallas_call(
        far_attention_kernel,
        grid=(steps,),
        in_specs=[
            block,
            pl.BlockSpec(bias.shape, lambda i: (0, 0)),
            *halves(one, steps),
            *halves(two, steps),
            block,
            pl.BlockSpec((quarter, HEAD), lambda i: (0, i)),
        ],
        out_specs=block,
        out_shape=jax.ShapeDtypeStruct((quarter, width), BF16),
        compiler_params=params(SMALL_LIMIT),
        name="far_attention",
    )(query, bias, one, one, two, two, summed, stats)


def finish_kernel(mixed_ref, last_ref, tiles_ref, weight_ref, finding_ref, mask_ref, layer_ref, keys_ref, stats_ref, plain_ref):
    slots, width = tiles_ref.shape
    quarter = slots // 4
    position = lax.broadcasted_iota(jnp.int32, (slots, slots), 0)
    index = lax.broadcasted_iota(jnp.int32, (slots, slots), 1)
    order = (original_of(index, quarter) == position).astype(F32).astype(BF16)
    for start in range(0, width, WIDE):
        heads = []
        for j in range(GROUP):
            cols = slice(start + j * HEAD, start + (j + 1) * HEAD)
            begin = QUARTER_OF[j] * quarter
            pieces = [last_ref[:, cols]]
            if begin > 0:
                pieces.insert(0, mixed_ref[:begin, cols])
            if begin + quarter < slots:
                pieces.append(mixed_ref[begin + quarter :, cols])
            heads.append(jnp.concatenate(pieces, axis=0))
        plain_ref[:, start : start + WIDE] = jnp.dot(
            order, jnp.concatenate(heads, axis=1), preferred_element_type=F32
        ).astype(BF16)
    square = jnp.zeros((slots, 1), F32)
    for start in range(0, width, WIDE):
        cols = slice(start, start + WIDE)
        added = jnp.dot(plain_ref[...], weight_ref[:, cols], preferred_element_type=F32)
        out = (tiles_ref[:, cols].astype(F32) + added).astype(BF16)
        layer_ref[:, cols] = out
        wide = out.astype(F32)
        square = square + jnp.sum(wide * wide, axis=1, keepdims=True)
    inverse = lax.rsqrt(square * (1.0 / width) + EPSILON)
    mask = mask_ref[...]
    for h in range(HEADS):
        cols = slice(h * HEAD, (h + 1) * HEAD)
        keys = (layer_ref[:, cols].astype(F32) * inverse).astype(BF16)
        keys_ref[:, cols] = keys
        scores = lax.dot_general(
            keys, finding_ref[:, cols], (((1,), (1,)), ((), ())), preferred_element_type=F32
        )
        scores = scores * FACTOR + mask
        peak = jnp.max(scores, axis=0, keepdims=True)
        stats_ref[h : h + 1, :] = peak
        stats_ref[HEADS + h : HEADS + h + 1, :] = jnp.sum(
            jnp.exp2(scores - peak), axis=0, keepdims=True
        )


def finish(mixed, last, tiles, weight, finding, mask):
    slots, width = tiles.shape
    return pl.pallas_call(
        finish_kernel,
        out_shape=(
            jax.ShapeDtypeStruct((slots, width), BF16),
            jax.ShapeDtypeStruct((slots, width), BF16),
            jax.ShapeDtypeStruct((2 * HEADS, finding.shape[0]), F32),
        ),
        scratch_shapes=[pltpu.VMEM((slots, width), BF16)],
        compiler_params=params(SMALL_LIMIT),
        name="finish",
    )(mixed, last, tiles, weight, finding, mask)


def heat_kernel(count, scale, stats_ref, keys_ref, finding_ref, mask_ref, heat_ref, held, kept, send_sem, recv_sem):
    slide = lax.axis_index("slide")
    me = lax.axis_index("seq")
    barrier = pltpu.get_barrier_semaphore()
    for hop in range(1, count):
        peer = lax.rem(me + hop, count)
        pl.semaphore_signal(
            barrier, inc=1, device_id=(slide, peer), device_id_type=pl.DeviceIdType.MESH
        )
    pl.semaphore_wait(barrier, count - 1)
    copies = []
    for hop in range(1, count):
        peer = lax.rem(me + hop, count)
        copy = pltpu.make_async_remote_copy(
            src_ref=stats_ref,
            dst_ref=held.at[hop],
            send_sem=send_sem.at[hop],
            recv_sem=recv_sem.at[hop],
            device_id=(slide, peer),
            device_id_type=pl.DeviceIdType.MESH,
        )
        copy.start()
        copies.append(copy)
    mask = mask_ref[...]
    for h in range(HEADS):
        cols = slice(h * HEAD, (h + 1) * HEAD)
        scores = lax.dot_general(
            keys_ref[:, cols], finding_ref[:, cols], (((1,), (1,)), ((), ())),
            preferred_element_type=F32,
        )
        kept[h] = jnp.exp2(scores * FACTOR + mask - stats_ref[h : h + 1, :])
    for copy in copies:
        copy.wait()
    everything = [stats_ref[...]] + [held[hop] for hop in range(1, count)]
    peaks = everything[0][:HEADS]
    for part in everything[1:]:
        peaks = jnp.maximum(peaks, part[:HEADS])
    totals = jnp.zeros_like(peaks)
    for part in everything:
        totals = totals + part[HEADS:] * jnp.exp2(part[:HEADS] - peaks)
    factors = jnp.exp2(everything[0][:HEADS] - peaks) * (scale / totals)
    slots = keys_ref.shape[0]
    chunk = 64
    for start in range(0, slots, chunk):
        rows = slice(start, start + chunk)
        total = kept[0, rows, :] * factors[0:1]
        for h in range(1, HEADS):
            total = total + kept[h, rows, :] * factors[h : h + 1]
        heat_ref[rows, :] = total


def heat_map(count, stats, keys, finding, mask):
    slots = keys.shape[0]
    finds = finding.shape[0]
    return pl.pallas_call(
        functools.partial(heat_kernel, count, count * slots / HEADS),
        in_specs=[pl.BlockSpec(memory_space=pltpu.VMEM)] * 4,
        out_specs=pl.BlockSpec(memory_space=pltpu.VMEM),
        out_shape=jax.ShapeDtypeStruct((slots, finds), F32),
        scratch_shapes=[
            pltpu.VMEM((count, 2 * HEADS, finds), F32),
            pltpu.VMEM((HEADS, slots, finds), F32),
            pltpu.SemaphoreType.DMA((count,)),
            pltpu.SemaphoreType.DMA((count,)),
        ],
        compiler_params=params(SMALL_LIMIT, collective_id=0, has_side_effects=True),
        name="heat_map",
    )(stats, keys, finding, mask)


def exchange(value, mask):
    pairs = [(source, source ^ mask) for source in range(lax.axis_size("seq"))]
    return lax.ppermute(value, "seq", pairs)


def shards(embeds, destination, norm_gain, qkv_weight, out_weight, finding_queries):
    devices = lax.axis_size(("slide", "seq"))
    seq_count = lax.axis_size("seq")
    slots = embeds.shape[0] * 2
    capacity = slots // devices
    padded = -(-capacity // 8) * 8
    width = embeds.shape[1]
    buffer, counts = dispatch(destination, embeds, devices, padded)
    received, counts = route(
        buffer.reshape(devices, padded, width), counts[None], devices, seq_count
    )
    tiles = received[:, :capacity].reshape(slots, width)
    pairs, near, far, normed, bias, mask = project(
        tiles, norm_gain, counts[:, 0], qkv_weight, capacity, seq_count
    )
    one = exchange(far, 2)
    pair = exchange(near, 1)
    query = project_query(normed, qkv_weight)
    mixed, summed, stats, quarter_query = near_attention(query, pairs, bias, pair)
    one, mixed = lax.optimization_barrier((one, mixed))
    two = exchange(one, 1)
    last = far_attention(quarter_query, bias, one, two, summed, stats)
    layer_out, keys, stats = finish(mixed, last, tiles, out_weight, finding_queries, mask)
    heat = heat_map(seq_count, stats, keys, finding_queries, mask)
    return (layer_out, heat)


def solution(mesh):
    in_specs = (P(("slide", "seq"), None), P(("slide", "seq"), None), P(), P(), P(), P())
    out_specs = (P(("slide", "seq"), None), P(("slide", "seq"), None))
    return jax.shard_map(shards, mesh=mesh, in_specs=in_specs, out_specs=out_specs, check_vma=False)
```
